32 devices in a mesh: group: 2 (over y), head: 4 (over z), cache: 4 (over x, core).
Axes of the slice: x: 2, y: 2, z: 4, core: 2. Of those that a mesh axis runs over, the one named last changes fastest.
Arguments:
- queries: bfloat16 [512, 4096], P(('group', 'head')), parts along dimension 0, may hold values from -8 to 8
- keys: bfloat16 [256, 128, 4096], P(('group', 'cache'), None, 'head'), parts along dimension 0, may hold values from -8 to 8
- values: bfloat16 [256, 128, 4096], P(('group', 'cache'), None, 'head'), parts along dimension 0, may hold values from -6 to 6
- page_lists: int32 [8, 32], P(('group', 'cache')), parts along dimension 0, may hold values from 0 to 31, as said below
- page_counts: int32 [8], P(('group', 'cache')), parts along dimension 0, may hold values from 1 to 32, as said below
Outputs:
- attended: float32 [512, 4096], P(('group', 'head', 'cache')), parts along dimension 0
- log_sums: float32 [512, 32], P(('group', 'head', 'cache')), parts along dimension 0
The draws below stay inside these ranges and needn't reach their ends.
There are 2 independent parts, one for each index of `group`. The reference program is written for one: setup_inputs(seed, part) draws one part's arguments, and reference() takes and returns one part's arrays. A program takes and returns all parts, laid end to end along the dimension named above; each array names one. Nothing has to cross between parts.
Inputs may be any that keep to these rules, and one draw needn't show every extreme that they name: `page_lists`: row c holds 32 distinct page ids of owner c's pool; only its first page_counts[c] entries are attended. `page_counts`: some owner lists exactly 32 pages in every draw.
All inputs are finite; a program needn't handle non-finite values.
Results may differ from the reference program's by a relative error of at most 0.00038.
Values may be sent and summed in bfloat16 or wider, within the bound.
A program may use at most 64 MiB of HBM per device.

```python
import math
import jax
import jax.numpy as jnp
from jax import lax

HEADS = 32
DH = 128
PAGE = 128
POOL = 32
MOST = 32
Q_TOK = 256
OWNERS = 4


def page_tables(key):
    base = jax.random.fold_in(key, 101)
    owner_keys = jax.random.split(jax.random.fold_in(base, 1), OWNERS)
    listed = jax.vmap(lambda owner_key: jax.random.permutation(owner_key, POOL)[:MOST])(owner_keys).astype(jnp.int32)
    counts = jax.random.randint(jax.random.fold_in(base, 2), (OWNERS,), 1, MOST // 2 + 1)
    busiest = jax.random.randint(jax.random.fold_in(base, 3), (), 0, OWNERS)
    counts = jnp.where(jnp.arange(OWNERS) == busiest, MOST, counts).astype(jnp.int32)
    return (listed, counts)


def drawn_draw(key, shape):
    return jnp.clip(1.7 * jax.random.normal(key, shape, jnp.float32), -8.0, 8.0)


def draw_page_lists(key, part):
    listed, counts = page_tables(key)
    return listed


def draw_page_counts(key, part):
    listed, counts = page_tables(key)
    return counts


def draw_queries(key, part):
    shape = (Q_TOK, HEADS * DH)
    drawn = drawn_draw(jax.random.fold_in(key, 304), shape)
    return drawn.astype(jnp.bfloat16)


def draw_keys(key, part):
    shape = (OWNERS * POOL, PAGE, HEADS * DH)
    drawn = drawn_draw(jax.random.fold_in(key, 405), shape)
    return drawn.astype(jnp.bfloat16)


def block_levels(stream_key, shape, cuts, smallest, largest):
    factor_of, own = 1.0, jax.random.fold_in(stream_key, 6)
    for position, blocks in cuts:
        steps = jnp.exp(jax.random.uniform(jax.random.fold_in(own, position), (blocks,), jnp.float32, smallest / len(cuts), largest / len(cuts)))
        factor_of = factor_of * jnp.repeat(steps, shape[position] // blocks).reshape([-1 if axis == position else 1 for axis in range(len(shape))])
    return factor_of


def scatter_about(key, dims, scale, most, shards=(), kind=jnp.bfloat16):
    result = scale * jax.random.normal(key, dims, jnp.float32)
    if shards:
        result = result * block_levels(key, dims, shards, -0.22, 0.18)
    return jnp.clip(result, -most, most).astype(kind)


def setup_inputs(seed: int = 0, part: int = 0) -> dict:
    arg_keys = jax.random.split(jax.random.key(seed), 6)
    part_keys = jax.random.split(jax.random.fold_in(arg_keys[5], part), 6)
    queries = draw_queries(jax.random.fold_in(jax.random.fold_in(arg_keys[5], part), 71), part)
    keys = draw_keys(jax.random.fold_in(jax.random.fold_in(arg_keys[5], part), 71), part)
    values = scatter_about(part_keys[2], (OWNERS * POOL, PAGE, HEADS * DH), 1.0, 6.0, ((0, 4), (2, 4)))
    page_lists = draw_page_lists(jax.random.fold_in(jax.random.fold_in(arg_keys[5], part), 71), part)
    page_counts = draw_page_counts(jax.random.fold_in(jax.random.fold_in(arg_keys[5], part), 71), part)
    return {"queries": queries, "keys": keys, "values": values, "page_lists": page_lists, "page_counts": page_counts}


lowest = -1e+30

def reference(queries, keys, values, page_lists, page_counts):
    score_scale = 1.0 / math.sqrt(DH)
    query_heads = queries.reshape(Q_TOK, HEADS, DH).astype(jnp.float32)
    owner_ids = jnp.arange(OWNERS, dtype=jnp.int32)
    page_rows = (owner_ids[:, None] * POOL + page_lists).reshape(-1).astype(jnp.int32)
    live = (jnp.arange(MOST, dtype=jnp.int32)[None, :] < page_counts[:, None]).reshape(-1)

    def update(state, row):
        best, total, accum = state
        key_page = lax.dynamic_index_in_dim(keys, row, 0, keepdims=False).reshape(PAGE, HEADS, DH).astype(jnp.float32)
        value_page = lax.dynamic_index_in_dim(values, row, 0, keepdims=False).reshape(PAGE, HEADS, DH).astype(jnp.float32)
        scores = jnp.einsum('thd,khd->thk', query_heads, key_page) * score_scale
        page_max = lax.optimization_barrier(jnp.max(scores, axis=-1))
        rounded = jnp.exp(scores - page_max[..., None]).astype(jnp.bfloat16)
        weights = lax.optimization_barrier(rounded).astype(jnp.float32)
        page_sum = lax.optimization_barrier(jnp.sum(weights, axis=-1))
        page_out = jnp.einsum('thk,khd->thd', weights, value_page)
        running = jnp.maximum(best, page_max)
        keep = jnp.exp(best - running)
        fresh = jnp.exp(page_max - running)
        return (running, total * keep + fresh * page_sum, accum * keep[..., None] + fresh[..., None] * page_out)

    def visit(state, item):
        row, used = item
        return (lax.cond(used, lambda inner: update(inner, row), lambda inner: inner, state), None)
    start = (jnp.full((Q_TOK, HEADS), lowest, jnp.float32), jnp.zeros((Q_TOK, HEADS), jnp.float32), jnp.zeros((Q_TOK, HEADS, DH), jnp.float32))
    (best, total, accum), _ = lax.scan(visit, start, (page_rows, live))
    attended = (accum / total[..., None]).reshape(Q_TOK, HEADS * DH)
    log_sums = best + jnp.log(total)
    return (attended, log_sums)
```

```python
import functools
import math

import jax
import jax.numpy as jnp
from jax import lax
from jax.experimental import pallas as pl
from jax.experimental.pallas import tpu as pltpu
from jax.sharding import PartitionSpec as P

DH = 128
PAGE = 128
LANES = 128
TILE = 256
ROWS = DH + 8
BLOCK = 4
SCALE = 1.0 / math.sqrt(DH)
LOG2_SCALE = SCALE * math.log2(math.e)

lowest = -1e30
highest = 3e38


def attend(query, key_of, value_of, caps, pages, acc):
    acc[...] = jnp.zeros_like(acc)
    ones = jnp.ones((16, PAGE), jnp.bfloat16)

    def visit(block, best):
        maxima, outs = [], []
        for step in range(BLOCK):
            page = block * BLOCK + step
            scores = lax.dot_general(
                key_of(page), query, (((1,), (1,)), ((), ())), preferred_element_type=jnp.float32
            )
            page_max = jnp.max(scores, axis=0, keepdims=True)
            weights = jnp.exp2((scores - page_max) * LOG2_SCALE).astype(jnp.bfloat16)
            left = jnp.concatenate([value_of(page).T, ones], axis=0)
            outs.append(jnp.dot(left, weights, preferred_element_type=jnp.float32)[:ROWS])
            maxima.append(jnp.minimum(page_max, caps[page]))
        running = functools.reduce(jnp.maximum, maxima, best)
        joined = acc[...] * jnp.exp2((best - running) * LOG2_SCALE)
        for used_max, out in zip(maxima, outs):
            joined += out * jnp.exp2((used_max - running) * LOG2_SCALE)
        acc[...] = joined
        return running

    start = jnp.full((1, TILE), lowest, jnp.float32)
    return lax.fori_loop(0, pages // BLOCK, visit, start)


def kernel(plan, q_ref, k_hbm, v_hbm, caps, out_ref, k_buf, v_buf, acc, k_sem, v_sem):
    groups, heads_in, tiles_in, tile_blocks, n_cache = plan
    width = heads_in * DH
    pages = k_hbm.shape[0]
    head_blocks = groups // tile_blocks

    def load(block):
        columns = pl.ds(block * width, width)
        return (
            pltpu.make_async_copy(k_hbm.at[:, :, columns], k_buf.at[block], k_sem.at[block]),
            pltpu.make_async_copy(v_hbm.at[:, :, columns], v_buf.at[block], v_sem.at[block]),
        )

    for block in range(head_blocks):
        for copy in load(block):
            copy.start()
    for block in range(head_blocks):
        for copy in load(block):
            copy.wait()
        for tile_block in range(tile_blocks):
            group = block * tile_blocks + tile_block
            bests = []
            for unit in range(heads_in * tiles_in):
                head = unit // tiles_in
                columns = slice(head * DH, (head + 1) * DH)
                best = attend(
                    q_ref[group * heads_in * tiles_in + unit],
                    lambda page: k_buf[block, page, :, columns],
                    lambda page: v_buf[block, page, :, columns],
                    caps, pages, acc.at[unit],
                )
                bests.append(best)
            chunk = TILE // n_cache
            row = lax.broadcasted_iota(jnp.int32, (ROWS, TILE), 0)
            whole = [
                jnp.where(row == DH + 1, best, acc[unit]) for unit, best in enumerate(bests)
            ]
            for member in range(n_cache):
                piece = slice(member * chunk, (member + 1) * chunk)
                out_ref[group, member] = jnp.concatenate([part[:, piece] for part in whole], axis=1)


def on_device(queries, keys, values, page_lists, page_counts):
    n_head = lax.axis_size("head")
    n_cache = lax.axis_size("cache")
    tok_local = queries.shape[0]
    heads = keys.shape[2] // DH
    pages = keys.shape[0]
    share = tok_local // n_cache
    sources = TILE // tok_local
    tiles = n_head // sources
    units = LANES * n_cache // TILE
    tiles_in = min(units, tiles)
    heads_in = units // tiles_in
    tile_blocks = tiles // tiles_in
    head_blocks = heads // heads_in
    groups = head_blocks * tile_blocks
    moved = lax.all_to_all(
        queries.reshape(tok_local, n_head, heads * DH), "head", split_axis=1, concat_axis=0, tiled=True
    )
    moved = moved.reshape(tile_blocks, tiles_in, sources, n_cache, share, head_blocks, heads_in, DH)
    moved = moved.transpose(5, 0, 6, 1, 3, 2, 4, 7).reshape(groups * units, TILE, DH)
    used = jnp.arange(page_lists.shape[1], dtype=jnp.int32) < page_counts[0]
    ids = jnp.arange(pages, dtype=jnp.int32)
    live = jnp.any((page_lists[0][None, :] == ids[:, None]) & used[None, :], axis=1)
    caps = jnp.where(live, highest, lowest).astype(jnp.float32)
    plan = (groups, heads_in, tiles_in, tile_blocks, n_cache)
    width = heads_in * DH
    parts = pl.pallas_call(
        functools.partial(kernel, plan),
        out_shape=jax.ShapeDtypeStruct((groups, n_cache, ROWS, LANES), jnp.float32),
        in_specs=[
            pl.BlockSpec(memory_space=pltpu.VMEM),
            pl.BlockSpec(memory_space=pl.ANY),
            pl.BlockSpec(memory_space=pl.ANY),
            pl.BlockSpec(memory_space=pltpu.SMEM),
        ],
        out_specs=pl.BlockSpec(memory_space=pltpu.VMEM),
        scratch_shapes=[
            pltpu.VMEM((head_blocks, pages, PAGE, width), jnp.bfloat16),
            pltpu.VMEM((head_blocks, pages, PAGE, width), jnp.bfloat16),
            pltpu.VMEM((units, ROWS, TILE), jnp.float32),
            pltpu.SemaphoreType.DMA((head_blocks,)),
            pltpu.SemaphoreType.DMA((head_blocks,)),
        ],
        compiler_params=pltpu.CompilerParams(vmem_limit_bytes=56 * 1024 * 1024),
    )(moved, keys, values, caps)
    parts = lax.all_to_all(parts, "cache", split_axis=1, concat_axis=1, tiled=True)
    accum, total, best = parts[:, :, :DH], parts[:, :, DH], parts[:, :, DH + 1]
    top = jnp.max(best, axis=1, keepdims=True)
    keep = jnp.exp2((best - top) * LOG2_SCALE)
    total = jnp.sum(total * keep, axis=1)
    result = jnp.sum(accum * keep[:, :, None], axis=1) / total[:, None]
    logged = top[:, 0] * SCALE + jnp.log(total)
    lanes = (heads_in, tiles_in, sources, share)
    result = result.reshape(head_blocks, tile_blocks, DH, *lanes).transpose(1, 4, 5, 6, 0, 3, 2)
    logged = logged.reshape(head_blocks, tile_blocks, *lanes).transpose(1, 3, 4, 5, 0, 2)
    result = result.reshape(n_head, share, heads * DH)
    logged = logged.reshape(n_head, share, heads)
    result = lax.all_to_all(result, "head", split_axis=0, concat_axis=2, tiled=True)
    logged = lax.all_to_all(logged, "head", split_axis=0, concat_axis=2, tiled=True)
    return (result.reshape(share, -1), logged.reshape(share, -1))


def solution(mesh):
    in_specs = (
        P(("group", "head"), None),
        P(("group", "cache"), None, "head"),
        P(("group", "cache"), None, "head"),
        P(("group", "cache"), None),
        P(("group", "cache")),
    )
    out_specs = (P(("group", "head", "cache"), None), P(("group", "head", "cache"), None))
    return jax.shard_map(
        on_device, mesh=mesh, in_specs=in_specs, out_specs=out_specs, check_vma=False
    )
```

```python
import functools
import math

import jax
import jax.numpy as jnp
from jax import lax
from jax.experimental import pallas as pl
from jax.experimental.pallas import tpu as pltpu
from jax.sharding import PartitionSpec as P

DH = 128
PAGE = 128
LANES = 128
TILE = 256
ROWS = DH + 8
BLOCK = 4
SCALE = 1.0 / math.sqrt(DH)
LOG2_SCALE = SCALE * math.log2(math.e)

lowest = -1e30
highest = 3e38


def attend(queries, key_of, value_of, caps, pages, acc, scores):
    units = len(queries)
    acc[...] = jnp.zeros_like(acc)
    ones = jnp.ones((16, PAGE), jnp.bfloat16)
    blocks = pages // BLOCK

    def score(unit, page):
        return lax.dot_general(
            key_of(unit, page), queries[unit][...], (((1,), (1,)), ((), ())),
            preferred_element_type=jnp.float32,
        )

    for unit in range(units):
        for step in range(BLOCK):
            scores[unit, step] = score(unit, step)

    def visit(block, bests):
        after = jnp.minimum(block + 1, blocks - 1) * BLOCK
        runnings = []
        for unit in range(units):
            maxima, outs = [], []
            for step in range(BLOCK):
                page = block * BLOCK + step
                page_max = jnp.max(scores[unit, step], axis=0, keepdims=True)
                weights = jnp.exp2((scores[unit, step] - page_max) * LOG2_SCALE).astype(jnp.bfloat16)
                scores[unit, step] = score(unit, after + step)
                left = jnp.concatenate([value_of(unit, page).T, ones], axis=0)
                outs.append(jnp.dot(left, weights, preferred_element_type=jnp.float32)[:ROWS])
                maxima.append(jnp.minimum(page_max, caps[page]))
            running = functools.reduce(jnp.maximum, maxima, bests[unit])
            joined = acc[unit] * jnp.exp2((bests[unit] - running) * LOG2_SCALE)
            for used_max, out in zip(maxima, outs):
                joined += out * jnp.exp2((used_max - running) * LOG2_SCALE)
            acc[unit] = joined
            runnings.append(running)
        return tuple(runnings)

    start = jnp.full((1, TILE), lowest, jnp.float32)
    return lax.fori_loop(0, blocks, visit, (start,) * units)


def kernel(
    plan, q_ref, k_hbm, v_hbm, caps, out_ref, log_ref,
    k_buf, v_buf, q_all, q_units, acc, scores, part_out, part_in, piece_out, piece_in, log_out, log_in,
    k_sem, v_sem, own_sem, q_send, q_recv, part_send, part_recv, piece_send, piece_recv, log_send, log_recv,
):
    groups, heads_in, tiles_in, tile_blocks, n_head, n_cache, heads, sources = plan
    units = heads_in * tiles_in
    width = heads_in * DH
    pages = k_hbm.shape[0]
    head_blocks = groups // tile_blocks
    share = q_ref.shape[0] // n_cache
    chunk = TILE // n_cache
    spread = tiles_in * sources
    me = lax.axis_index("head")
    seat = lax.axis_index("cache")

    def load(block):
        columns = pl.ds(pl.multiple_of(block * width, DH), width)
        return (
            pltpu.make_async_copy(k_hbm.at[:, :, columns], k_buf.at[block], k_sem.at[block]),
            pltpu.make_async_copy(v_hbm.at[:, :, columns], v_buf.at[block], v_sem.at[block]),
        )

    def peer_of(index, count, offset):
        return lax.rem(index + offset, count)

    def query_source(block, owner):
        return q_ref.at[:, pl.ds(pl.multiple_of(owner * heads * DH + block * width, DH), width)]

    def own_query(block):
        return pltpu.make_async_copy(query_source(block, me), q_all.at[block, me], own_sem.at[block])

    def query_copy(block, offset, source):
        peer = peer_of(me, n_head, offset)
        return pltpu.make_async_remote_copy(
            src_ref=query_source(block, peer), dst_ref=q_all.at[block, source],
            send_sem=q_send.at[block, offset - 1], recv_sem=q_recv.at[block, source],
            device_id={"head": peer}, device_id_type=pl.DeviceIdType.MESH,
        )

    def part_copy(group, offset, source):
        peer = peer_of(seat, n_cache, offset)
        return pltpu.make_async_remote_copy(
            src_ref=part_out.at[group, peer], dst_ref=part_in.at[group, source],
            send_sem=part_send.at[group, offset - 1], recv_sem=part_recv.at[group, source],
            device_id={"cache": peer}, device_id_type=pl.DeviceIdType.MESH,
        )

    def piece_copy(group, place, source):
        target = group % tile_blocks * spread + place
        block = group // tile_blocks
        return target, pltpu.make_async_remote_copy(
            src_ref=piece_out.at[group, place], dst_ref=piece_in.at[block, source],
            send_sem=piece_send.at[group, place], recv_sem=piece_recv.at[block, source],
            device_id={"head": target}, device_id_type=pl.DeviceIdType.MESH,
        )

    def log_copy(offset, source):
        peer = peer_of(me, n_head, offset)
        return pltpu.make_async_remote_copy(
            src_ref=log_out.at[peer], dst_ref=log_in.at[source],
            send_sem=log_send.at[offset - 1], recv_sem=log_recv.at[source],
            device_id={"head": peer}, device_id_type=pl.DeviceIdType.MESH,
        )

    for copy in load(0):
        copy.start()
    barrier = pltpu.get_barrier_semaphore()
    for offset in range(1, n_head):
        pl.semaphore_signal(
            barrier, inc=1, device_id={"head": peer_of(me, n_head, offset)},
            device_id_type=pl.DeviceIdType.MESH,
        )
    for offset in range(1, n_cache):
        pl.semaphore_signal(
            barrier, inc=1, device_id={"cache": peer_of(seat, n_cache, offset)},
            device_id_type=pl.DeviceIdType.MESH,
        )
    for block in range(head_blocks):
        own_query(block).start()
        if block:
            for copy in load(block):
                copy.start()
    pl.semaphore_wait(barrier, n_head + n_cache - 2)
    for block in range(head_blocks):
        for offset in range(1, n_head):
            query_copy(block, offset, me).start()
    log_out[...] = jnp.zeros_like(log_out)

    def ready(block):
        for copy in load(block):
            copy.wait()
        own_query(block).wait()
        for offset in range(1, n_head):
            query_copy(block, offset, peer_of(me, n_head, offset)).wait_recv()

    def compute(group):
        block = group // tile_blocks
        if tile_blocks == 1:
            ready(block)
        else:
            pl.when(group % tile_blocks == 0)(lambda: ready(block))

        def column(unit):
            return slice(unit // tiles_in * DH, (unit // tiles_in + 1) * DH)

        for unit in range(units):
            first = (group % tile_blocks * tiles_in + unit % tiles_in) * sources
            rows = [q_all[block, first + l, :, column(unit)].astype(jnp.float32) for l in range(sources)]
            ordered = [
                row[c * share:(c + 1) * share] for c in range(n_cache) for row in rows
            ]
            q_units[unit] = jnp.concatenate(ordered, axis=0).astype(jnp.bfloat16)
        bests = attend(
            [q_units.at[unit] for unit in range(units)],
            lambda unit, page: k_buf[block, page, :, column(unit)],
            lambda unit, page: v_buf[block, page, :, column(unit)],
            caps, pages, acc, scores,
        )
        row = lax.broadcasted_iota(jnp.int32, (8, TILE), 0)
        tails = [jnp.where(row == 1, best, acc[unit, DH:ROWS]) for unit, best in enumerate(bests)]
        for member in range(n_cache):
            piece = slice(member * chunk, (member + 1) * chunk)
            part_out[group, member, :DH] = jnp.concatenate(
                [acc[unit, :DH, piece] for unit in range(units)], axis=1
            )
            part_out[group, member, DH:ROWS] = jnp.concatenate([tail[:, piece] for tail in tails], axis=1)
        for offset in range(1, n_cache):
            part_copy(group, offset, seat).start()
        part_in[group, seat] = part_out[group, seat]

    def finish(group):
        block = group // tile_blocks
        for offset in range(1, n_cache):
            part_copy(group, offset, peer_of(seat, n_cache, offset)).wait_recv()
        totals = [part_in[group, c, DH:DH + 1] for c in range(n_cache)]
        bests = [part_in[group, c, DH + 1:DH + 2] for c in range(n_cache)]
        top = functools.reduce(jnp.maximum, bests)
        keeps = [jnp.exp2((best - top) * LOG2_SCALE) for best in bests]
        total = functools.reduce(jnp.add, [t * keep for t, keep in zip(totals, keeps)])
        inverse = 1.0 / total
        result = functools.reduce(
            jnp.add, [part_in[group, c, :DH] * (keep * inverse) for c, keep in enumerate(keeps)]
        ).T
        logged = jnp.broadcast_to(top * SCALE + jnp.log(total), (LANES, LANES)).T
        lane = lax.broadcasted_iota(jnp.int32, (share, LANES), 1)
        for unit in range(units):
            head = unit // tiles_in
            for l in range(sources):
                place = unit % tiles_in * sources + l
                at = unit * sources * share + l * share
                piece_out[group, place, :, head * DH:(head + 1) * DH] = result[at:at + share]
                target = group % tile_blocks * spread + place
                log_out[target] += jnp.where(
                    lane == me * heads + block * heads_in + head, logged[at:at + share], 0.0
                )
        for place in range(spread):
            target, copy = piece_copy(group, place, me)
            pl.when(target != me)(copy.start)

            @pl.when(target == me)
            def _():
                piece_in[block, me] = piece_out[group, place]

    compute(0)

    def step(group, carry):
        compute(group)
        finish(group - 1)
        return carry

    lax.fori_loop(1, groups, step, 0)
    finish(groups - 1)
    for offset in range(1, n_head):
        log_copy(offset, me).start()
    log_in[me] = log_out[me]
    for block in range(head_blocks):
        for offset in range(1, n_head):
            query_copy(block, offset, me).wait_send()
    for group in range(groups):
        for offset in range(1, n_cache):
            part_copy(group, offset, seat).wait_send()
    for block in range(head_blocks):
        for offset in range(1, n_head):
            source = peer_of(me, n_head, offset)
            pltpu.make_async_remote_copy(
                src_ref=piece_out.at[block, 0], dst_ref=piece_in.at[block, source],
                send_sem=piece_send.at[block, 0], recv_sem=piece_recv.at[block, source],
                device_id={"head": source}, device_id_type=pl.DeviceIdType.MESH,
            ).wait_recv()
        for source in range(n_head):
            at = (source * heads + block * heads_in) * DH
            out_ref[:, at:at + width] = piece_in[block, source]
    for offset in range(1, n_head):
        log_copy(offset, peer_of(me, n_head, offset)).wait_recv()
    log_ref[...] = functools.reduce(jnp.add, [log_in[s] for s in range(n_head)])[:, :log_ref.shape[1]]
    for group in range(groups):
        for place in range(spread):
            target, copy = piece_copy(group, place, me)
            pl.when(target != me)(copy.wait_send)
    for offset in range(1, n_head):
        log_copy(offset, me).wait_send()


def on_device(queries, keys, values, page_lists, page_counts):
    n_head = lax.axis_size("head")
    n_cache = lax.axis_size("cache")
    tok_local = queries.shape[0]
    heads = keys.shape[2] // DH
    pages = keys.shape[0]
    share = tok_local // n_cache
    sources = TILE // tok_local
    tiles = n_head // sources
    units = LANES * n_cache // TILE
    tiles_in = min(units, tiles)
    heads_in = units // tiles_in
    tile_blocks = tiles // tiles_in
    head_blocks = heads // heads_in
    groups = head_blocks * tile_blocks
    spread = tiles_in * sources
    width = heads_in * DH
    used = jnp.arange(page_lists.shape[1], dtype=jnp.int32) < page_counts[0]
    ids = jnp.arange(pages, dtype=jnp.int32)
    live = jnp.any((page_lists[0][None, :] == ids[:, None]) & used[None, :], axis=1)
    caps = jnp.where(live, highest, lowest).astype(jnp.float32)
    plan = (groups, heads_in, tiles_in, tile_blocks, n_head, n_cache, heads, sources)
    dma = pltpu.SemaphoreType.DMA
    return pl.pallas_call(
        functools.partial(kernel, plan),
        out_shape=(
            jax.ShapeDtypeStruct((share, queries.shape[1]), jnp.float32),
            jax.ShapeDtypeStruct((share, n_head * heads), jnp.float32),
        ),
        in_specs=[
            pl.BlockSpec(memory_space=pltpu.VMEM),
            pl.BlockSpec(memory_space=pl.ANY),
            pl.BlockSpec(memory_space=pl.ANY),
            pl.BlockSpec(memory_space=pltpu.SMEM),
        ],
        out_specs=(pl.BlockSpec(memory_space=pltpu.VMEM), pl.BlockSpec(memory_space=pltpu.VMEM)),
        scratch_shapes=[
            pltpu.VMEM((head_blocks, pages, PAGE, width), jnp.bfloat16),
            pltpu.VMEM((head_blocks, pages, PAGE, width), jnp.bfloat16),
            pltpu.VMEM((head_blocks, n_head, tok_local, width), jnp.bfloat16),
            pltpu.VMEM((units, TILE, DH), jnp.bfloat16),
            pltpu.VMEM((units, ROWS, TILE), jnp.float32),
            pltpu.VMEM((units, BLOCK, PAGE, TILE), jnp.float32),
            pltpu.VMEM((groups, n_cache, ROWS, LANES), jnp.float32),
            pltpu.VMEM((groups, n_cache, ROWS, LANES), jnp.float32),
            pltpu.VMEM((groups, spread, share, width), jnp.float32),
            pltpu.VMEM((head_blocks, n_head, share, width), jnp.float32),
            pltpu.VMEM((n_head, share, LANES), jnp.float32),
            pltpu.VMEM((n_head, share, LANES), jnp.float32),
            dma((head_blocks,)),
            dma((head_blocks,)),
            dma((head_blocks,)),
            dma((head_blocks, n_head - 1)),
            dma((head_blocks, n_head)),
            dma((groups, n_cache - 1)),
            dma((groups, n_cache)),
            dma((groups, spread)),
            dma((head_blocks, n_head)),
            dma((n_head - 1,)),
            dma((n_head,)),
        ],
        compiler_params=pltpu.CompilerParams(
            collective_id=0, has_side_effects=True, vmem_limit_bytes=56 * 1024 * 1024
        ),
    )(queries, keys, values, caps)


def solution(mesh):
    in_specs = (
        P(("group", "head"), None),
        P(("group", "cache"), None, "head"),
        P(("group", "cache"), None, "head"),
        P(("group", "cache"), None),
        P(("group", "cache")),
    )
    out_specs = (P(("group", "head", "cache"), None), P(("group", "head", "cache"), None))
    return jax.shard_map(
        on_device, mesh=mesh, in_specs=in_specs, out_specs=out_specs, check_vma=False
    )
```

```python
import functools
import math

import jax
import jax.numpy as jnp
from jax import lax
from jax.experimental import pallas as pl
from jax.experimental.pallas import tpu as pltpu
from jax.sharding import PartitionSpec as P

DH = 128
PAGE = 128
LANES = 128
TILE = 256
ROWS = DH + 8
BLOCK = 8
SCALE = 1.0 / math.sqrt(DH)
LOG2_SCALE = SCALE * math.log2(math.e)

lowest = -1e30
highest = 3e38


def attend(queries, key_of, value_of, caps, pages, acc, scores):
    units = len(queries)
    acc[...] = jnp.zeros_like(acc)
    ones = jnp.ones((16, PAGE), jnp.bfloat16)
    blocks = pages // BLOCK

    def score(unit, page):
        rows = key_of(unit, pl.ds(page, BLOCK)).reshape(BLOCK * PAGE, DH)
        return lax.dot_general(
            rows, queries[unit][...], (((1,), (1,)), ((), ())),
            preferred_element_type=jnp.float32,
        ).reshape(BLOCK, PAGE, TILE)

    for unit in range(units):
        scores[unit] = score(unit, 0)

    def visit(block, bests, more=True):
        runnings = []
        for unit in range(units):
            maxima, outs = [], []
            for step in range(BLOCK):
                page = block * BLOCK + step
                page_max = jnp.max(scores[unit, step], axis=0, keepdims=True)
                weights = jnp.exp2((scores[unit, step] - page_max) * LOG2_SCALE).astype(jnp.bfloat16)
                left = jnp.concatenate([value_of(unit, page).T, ones], axis=0)
                outs.append(jnp.dot(left, weights, preferred_element_type=jnp.float32)[:ROWS])
                maxima.append(jnp.minimum(page_max, caps[pl.ds(page, 1), :]))
            if more:
                scores[unit] = score(unit, (block + 1) * BLOCK)
            running = functools.reduce(jnp.maximum, maxima, bests[unit])
            joined = acc[unit] * jnp.exp2((bests[unit] - running) * LOG2_SCALE)
            for used_max, out in zip(maxima, outs):
                joined += out * jnp.exp2((used_max - running) * LOG2_SCALE)
            acc[unit] = joined
            runnings.append(running)
        return tuple(runnings)

    start = jnp.full((1, TILE), lowest, jnp.float32)
    bests = lax.fori_loop(0, blocks - 1, visit, (start,) * units)
    return visit(blocks - 1, bests, more=False)


def kernel(
    plan, q_ref, k_hbm, v_hbm, lists, counts, out_ref, log_ref,
    caps, k_buf, v_buf, q_all, q_units, acc, scores, part_out, part_in, piece_out, piece_in, log_out, log_in,
    k_sem, v_sem, own_sem, q_send, q_recv, part_send, part_recv, piece_send, piece_recv, log_send, log_recv,
):
    groups, heads_in, tiles_in, tile_blocks, n_head, n_cache, heads, sources = plan
    units = heads_in * tiles_in
    width = heads_in * DH
    pages = k_hbm.shape[0]
    head_blocks = groups // tile_blocks
    share = q_ref.shape[0] // n_cache
    chunk = TILE // n_cache
    spread = tiles_in * sources
    me = lax.axis_index("head")
    seat = lax.axis_index("cache")

    def load(block):
        columns = pl.ds(pl.multiple_of(block * width, DH), width)
        return (
            pltpu.make_async_copy(k_hbm.at[:, :, columns], k_buf.at[block], k_sem.at[block]),
            pltpu.make_async_copy(v_hbm.at[:, :, columns], v_buf.at[block], v_sem.at[block]),
        )

    def peer_of(index, count, offset):
        return lax.rem(index + offset, count)

    def query_source(block, owner):
        return q_ref.at[:, pl.ds(pl.multiple_of(owner * heads * DH + block * width, DH), width)]

    def own_query(block):
        return pltpu.make_async_copy(query_source(block, me), q_all.at[block, me], own_sem.at[block])

    def query_copy(block, offset, source):
        peer = peer_of(me, n_head, offset)
        return pltpu.make_async_remote_copy(
            src_ref=query_source(block, peer), dst_ref=q_all.at[block, source],
            send_sem=q_send.at[block, offset - 1], recv_sem=q_recv.at[block, source],
            device_id={"head": peer}, device_id_type=pl.DeviceIdType.MESH,
        )

    def part_copy(group, offset, source):
        peer = peer_of(seat, n_cache, offset)
        return pltpu.make_async_remote_copy(
            src_ref=part_out.at[group, peer], dst_ref=part_in.at[group, source],
            send_sem=part_send.at[group, offset - 1], recv_sem=part_recv.at[group, source],
            device_id={"cache": peer}, device_id_type=pl.DeviceIdType.MESH,
        )

    def piece_copy(group, place, source):
        target = group % tile_blocks * spread + place
        block = group // tile_blocks
        return target, pltpu.make_async_remote_copy(
            src_ref=piece_out.at[group, place], dst_ref=piece_in.at[block, source],
            send_sem=piece_send.at[group, place], recv_sem=piece_recv.at[block, source],
            device_id={"head": target}, device_id_type=pl.DeviceIdType.MESH,
        )

    def log_copy(offset, source):
        peer = peer_of(me, n_head, offset)
        return pltpu.make_async_remote_copy(
            src_ref=log_out.at[peer], dst_ref=log_in.at[source],
            send_sem=log_send.at[offset - 1], recv_sem=log_recv.at[source],
            device_id={"head": peer}, device_id_type=pl.DeviceIdType.MESH,
        )

    for copy in load(0):
        copy.start()
    barrier = pltpu.get_barrier_semaphore()
    for offset in range(1, n_head):
        pl.semaphore_signal(
            barrier, inc=1, device_id={"head": peer_of(me, n_head, offset)},
            device_id_type=pl.DeviceIdType.MESH,
        )
    for offset in range(1, n_cache):
        pl.semaphore_signal(
            barrier, inc=1, device_id={"cache": peer_of(seat, n_cache, offset)},
            device_id_type=pl.DeviceIdType.MESH,
        )
    for block in range(head_blocks):
        own_query(block).start()
        if block:
            for copy in load(block):
                copy.start()
    pl.semaphore_wait(barrier, n_head + n_cache - 2)
    for block in range(head_blocks):
        for offset in range(1, n_head):
            query_copy(block, offset, me).start()
    log_out[...] = jnp.zeros_like(log_out)
    slots = lists.shape[1]
    used = lax.broadcasted_iota(jnp.int32, (1, slots), 1) < counts[0]
    listed = jnp.where(used, lists[...], -1)
    match = listed == lax.broadcasted_iota(jnp.int32, (pages, slots), 0)
    cap = jnp.max(jnp.where(match, highest, lowest), axis=1, keepdims=True)
    caps[...] = jnp.broadcast_to(cap, caps.shape)

    def ready(block):
        for copy in load(block):
            copy.wait()
        own_query(block).wait()
        for offset in range(1, n_head):
            query_copy(block, offset, peer_of(me, n_head, offset)).wait_recv()

    def compute(group):
        block = group // tile_blocks
        if tile_blocks == 1:
            ready(block)
        else:
            pl.when(group % tile_blocks == 0)(lambda: ready(block))

        def column(unit):
            return slice(unit // tiles_in * DH, (unit // tiles_in + 1) * DH)

        for unit in range(units):
            first = (group % tile_blocks * tiles_in + unit % tiles_in) * sources
            rows = [q_all[block, first + l, :, column(unit)].astype(jnp.float32) for l in range(sources)]
            ordered = [
                row[c * share:(c + 1) * share] for c in range(n_cache) for row in rows
            ]
            q_units[unit] = jnp.concatenate(ordered, axis=0).astype(jnp.bfloat16)
        bests = attend(
            [q_units.at[unit] for unit in range(units)],
            lambda unit, page: k_buf[block, page, :, column(unit)],
            lambda unit, page: v_buf[block, page, :, column(unit)],
            caps, pages, acc, scores,
        )
        row = lax.broadcasted_iota(jnp.int32, (8, TILE), 0)
        tails = [jnp.where(row == 1, best, acc[unit, DH:ROWS]) for unit, best in enumerate(bests)]
        for member in range(n_cache):
            piece = slice(member * chunk, (member + 1) * chunk)
            part_out[group, member, :DH] = jnp.concatenate(
                [acc[unit, :DH, piece] for unit in range(units)], axis=1
            )
            part_out[group, member, DH:ROWS] = jnp.concatenate([tail[:, piece] for tail in tails], axis=1)
        for offset in range(1, n_cache):
            part_copy(group, offset, seat).start()
        part_in[group, seat] = part_out[group, seat]

    def finish(group):
        block = group // tile_blocks
        for offset in range(1, n_cache):
            part_copy(group, offset, peer_of(seat, n_cache, offset)).wait_recv()
        totals = [part_in[group, c, DH:DH + 1] for c in range(n_cache)]
        bests = [part_in[group, c, DH + 1:DH + 2] for c in range(n_cache)]
        top = functools.reduce(jnp.maximum, bests)
        keeps = [jnp.exp2((best - top) * LOG2_SCALE) for best in bests]
        total = functools.reduce(jnp.add, [t * keep for t, keep in zip(totals, keeps)])
        inverse = 1.0 / total
        result = functools.reduce(
            jnp.add, [part_in[group, c, :DH] * (keep * inverse) for c, keep in enumerate(keeps)]
        ).T
        logged = jnp.broadcast_to(top * SCALE + jnp.log(total), (LANES, LANES)).T
        lane = lax.broadcasted_iota(jnp.int32, (share, LANES), 1)
        for unit in range(units):
            head = unit // tiles_in
            for l in range(sources):
                place = unit % tiles_in * sources + l
                at = unit * sources * share + l * share
                piece_out[group, place, :, head * DH:(head + 1) * DH] = result[at:at + share]
                target = group % tile_blocks * spread + place
                log_out[target] += jnp.where(
                    lane == me * heads + block * heads_in + head, logged[at:at + share], 0.0
                )
        for place in range(spread):
            target, copy = piece_copy(group, place, me)
            pl.when(target != me)(copy.start)

            @pl.when(target == me)
            def _():
                piece_in[block, me] = piece_out[group, place]

    def step(group, carry):
        compute(group)
        pl.when(group > 0)(lambda: finish(group - 1))
        return carry

    lax.fori_loop(0, groups, step, 0)
    finish(groups - 1)
    for offset in range(1, n_head):
        log_copy(offset, me).start()
    log_in[me] = log_out[me]
    for block in range(head_blocks):
        for offset in range(1, n_head):
            query_copy(block, offset, me).wait_send()
    for group in range(groups):
        for offset in range(1, n_cache):
            part_copy(group, offset, seat).wait_send()
    for block in range(head_blocks):
        for offset in range(1, n_head):
            source = peer_of(me, n_head, offset)
            pltpu.make_async_remote_copy(
                src_ref=piece_out.at[block, 0], dst_ref=piece_in.at[block, source],
                send_sem=piece_send.at[block, 0], recv_sem=piece_recv.at[block, source],
                device_id={"head": source}, device_id_type=pl.DeviceIdType.MESH,
            ).wait_recv()
        for source in range(n_head):
            at = (source * heads + block * heads_in) * DH
            out_ref[:, at:at + width] = piece_in[block, source]
    for offset in range(1, n_head):
        log_copy(offset, peer_of(me, n_head, offset)).wait_recv()
    log_ref[...] = functools.reduce(jnp.add, [log_in[s] for s in range(n_head)])[:, :log_ref.shape[1]]
    for group in range(groups):
        for place in range(spread):
            target, copy = piece_copy(group, place, me)
            pl.when(target != me)(copy.wait_send)
    for offset in range(1, n_head):
        log_copy(offset, me).wait_send()


def settle(attended, logged, out_ref, log_ref, sem):
    copies = (
        pltpu.make_async_copy(attended, out_ref, sem.at[0]),
        pltpu.make_async_copy(logged, log_ref, sem.at[1]),
    )
    for copy in copies:
        copy.start()
    for copy in copies:
        copy.wait()


def on_device(queries, keys, values, page_lists, page_counts):
    n_head = lax.axis_size("head")
    n_cache = lax.axis_size("cache")
    tok_local = queries.shape[0]
    heads = keys.shape[2] // DH
    pages = keys.shape[0]
    share = tok_local // n_cache
    sources = TILE // tok_local
    tiles = n_head // sources
    units = LANES * n_cache // TILE
    tiles_in = min(units, tiles)
    heads_in = units // tiles_in
    tile_blocks = tiles // tiles_in
    head_blocks = heads // heads_in
    groups = head_blocks * tile_blocks
    spread = tiles_in * sources
    width = heads_in * DH
    plan = (groups, heads_in, tiles_in, tile_blocks, n_head, n_cache, heads, sources)
    dma = pltpu.SemaphoreType.DMA
    attended, logged = pl.pallas_call(
        functools.partial(kernel, plan),
        out_shape=(
            jax.ShapeDtypeStruct((share, queries.shape[1]), jnp.float32),
            jax.ShapeDtypeStruct((share, n_head * heads), jnp.float32),
        ),
        in_specs=[
            pl.BlockSpec(memory_space=pltpu.VMEM),
            pl.BlockSpec(memory_space=pl.ANY),
            pl.BlockSpec(memory_space=pl.ANY),
            pl.BlockSpec(memory_space=pltpu.VMEM),
            pl.BlockSpec(memory_space=pltpu.SMEM),
        ],
        out_specs=(pl.BlockSpec(memory_space=pltpu.VMEM), pl.BlockSpec(memory_space=pltpu.VMEM)),
        scratch_shapes=[
            pltpu.VMEM((pages, TILE), jnp.float32),
            pltpu.VMEM((head_blocks, pages, PAGE, width), jnp.bfloat16),
            pltpu.VMEM((head_blocks, pages, PAGE, width), jnp.bfloat16),
            pltpu.VMEM((head_blocks, n_head, tok_local, width), jnp.bfloat16),
            pltpu.VMEM((units, TILE, DH), jnp.bfloat16),
            pltpu.VMEM((units, ROWS, TILE), jnp.float32),
            pltpu.VMEM((units, BLOCK, PAGE, TILE), jnp.float32),
            pltpu.VMEM((groups, n_cache, ROWS, LANES), jnp.float32),
            pltpu.VMEM((groups, n_cache, ROWS, LANES), jnp.float32),
            pltpu.VMEM((groups, spread, share, width), jnp.float32),
            pltpu.VMEM((head_blocks, n_head, share, width), jnp.float32),
            pltpu.VMEM((n_head, share, LANES), jnp.float32),
            pltpu.VMEM((n_head, share, LANES), jnp.float32),
            dma((head_blocks,)),
            dma((head_blocks,)),
            dma((head_blocks,)),
            dma((head_blocks, n_head - 1)),
            dma((head_blocks, n_head)),
            dma((groups, n_cache - 1)),
            dma((groups, n_cache)),
            dma((groups, spread)),
            dma((head_blocks, n_head)),
            dma((n_head - 1,)),
            dma((n_head,)),
        ],
        compiler_params=pltpu.CompilerParams(
            collective_id=0, has_side_effects=True, vmem_limit_bytes=56 * 1024 * 1024
        ),
    )(queries, keys, values, page_lists, page_counts)
    any_place = pl.BlockSpec(memory_space=pl.ANY)
    return pl.pallas_call(
        settle,
        out_shape=(
            jax.ShapeDtypeStruct(attended.shape, jnp.float32),
            jax.ShapeDtypeStruct(logged.shape, jnp.float32),
        ),
        in_specs=[pl.BlockSpec(memory_space=pltpu.VMEM)] * 2,
        out_specs=(any_place, any_place),
        scratch_shapes=[dma((2,))],
    )(attended, logged)


def solution(mesh):
    in_specs = (
        P(("group", "head"), None),
        P(("group", "cache"), None, "head"),
        P(("group", "cache"), None, "head"),
        P(("group", "cache"), None),
        P(("group", "cache")),
    )
    out_specs = (P(("group", "head", "cache"), None), P(("group", "head", "cache"), None))
    return jax.shard_map(
        on_device, mesh=mesh, in_specs=in_specs, out_specs=out_specs, check_vma=False
    )
```

```python
import functools
import math

import jax
import jax.numpy as jnp
from jax import lax
from jax.experimental import pallas as pl
from jax.experimental.pallas import tpu as pltpu
from jax.sharding import PartitionSpec as P

DH = 128
PAGE = 128
LANES = 128
TILE = 256
ROWS = DH + 8
BLOCK = 8
SCALE = 1.0 / math.sqrt(DH)
LOG2_SCALE = SCALE * math.log2(math.e)

lowest = -1e30
highest = 3e38


def attend(queries, key_of, value_of, caps, pages, acc, scores):
    units = len(queries)
    acc[...] = jnp.zeros_like(acc)
    ones = jnp.ones((16, PAGE), jnp.bfloat16)
    blocks = pages // BLOCK

    def score(unit, page):
        rows = key_of(unit, pl.ds(page, BLOCK)).reshape(BLOCK * PAGE, DH)
        return lax.dot_general(
            rows, queries[unit][...], (((1,), (1,)), ((), ())),
            preferred_element_type=jnp.float32,
        ).reshape(BLOCK, PAGE, TILE)

    for unit in range(units):
        scores[unit] = score(unit, 0)

    def visit(block, bests, more=True):
        runnings = []
        for unit in range(units):
            maxima, outs = [], []
            for step in range(BLOCK):
                page = block * BLOCK + step
                page_max = jnp.max(scores[unit, step], axis=0, keepdims=True)
                weights = jnp.exp2((scores[unit, step] - page_max) * LOG2_SCALE).astype(jnp.bfloat16)
                left = jnp.concatenate([value_of(unit, page).T, ones], axis=0)
                outs.append(jnp.dot(left, weights, preferred_element_type=jnp.float32)[:ROWS])
                maxima.append(jnp.minimum(page_max, caps[pl.ds(page, 1), :]))
            if more:
                scores[unit] = score(unit, (block + 1) * BLOCK)
            running = functools.reduce(jnp.maximum, maxima, bests[unit])
            joined = acc[unit] * jnp.exp2((bests[unit] - running) * LOG2_SCALE)
            for used_max, out in zip(maxima, outs):
                joined += out * jnp.exp2((used_max - running) * LOG2_SCALE)
            acc[unit] = joined
            runnings.append(running)
        return tuple(runnings)

    start = jnp.full((1, TILE), lowest, jnp.float32)
    bests = lax.fori_loop(0, blocks - 1, visit, (start,) * units)
    return visit(blocks - 1, bests, more=False)


def kernel(
    plan, q_ref, k_hbm, v_hbm, lists, counts, out_ref, log_ref,
    caps, k_buf, v_buf, q_all, q_units, acc, scores, part_out, part_in, piece_out, piece_in, log_out, log_in,
    k_sem, v_sem, own_sem, q_send, q_recv, part_send, part_recv, piece_send, piece_recv, log_send, log_recv,
):
    groups, heads_in, tiles_in, tile_blocks, n_head, n_cache, heads, sources = plan
    units = heads_in * tiles_in
    width = heads_in * DH
    pages = k_hbm.shape[0]
    head_blocks = groups // tile_blocks
    share = q_ref.shape[0] // n_cache
    chunk = TILE // n_cache
    spread = tiles_in * sources
    me = lax.axis_index("head")
    seat = lax.axis_index("cache")

    def load(block):
        columns = pl.ds(pl.multiple_of(block * width, DH), width)
        return (
            pltpu.make_async_copy(k_hbm.at[:, :, columns], k_buf.at[block], k_sem.at[block]),
            pltpu.make_async_copy(v_hbm.at[:, :, columns], v_buf.at[block], v_sem.at[block]),
        )

    def peer_of(index, count, offset):
        return lax.rem(index + offset, count)

    def query_source(block, owner):
        return q_ref.at[:, pl.ds(pl.multiple_of(owner * heads * DH + block * width, DH), width)]

    def own_query(block):
        return pltpu.make_async_copy(query_source(block, me), q_all.at[block, me], own_sem.at[block])

    def query_copy(block, offset, source):
        peer = peer_of(me, n_head, offset)
        return pltpu.make_async_remote_copy(
            src_ref=query_source(block, peer), dst_ref=q_all.at[block, source],
            send_sem=q_send.at[block, offset - 1], recv_sem=q_recv.at[block, source],
            device_id={"head": peer}, device_id_type=pl.DeviceIdType.MESH,
        )

    def part_copy(group, offset, source):
        peer = peer_of(seat, n_cache, offset)
        return pltpu.make_async_remote_copy(
            src_ref=part_out.at[group, peer], dst_ref=part_in.at[group, source],
            send_sem=part_send.at[group, offset - 1], recv_sem=part_recv.at[group, source],
            device_id={"cache": peer}, device_id_type=pl.DeviceIdType.MESH,
        )

    def piece_copy(group, place, source):
        target = group % tile_blocks * spread + place
        block = group // tile_blocks
        return target, pltpu.make_async_remote_copy(
            src_ref=piece_out.at[group, place], dst_ref=piece_in.at[block, source],
            send_sem=piece_send.at[group, place], recv_sem=piece_recv.at[block, source],
            device_id={"head": target}, device_id_type=pl.DeviceIdType.MESH,
        )

    def log_copy(offset, source):
        peer = peer_of(me, n_head, offset)
        return pltpu.make_async_remote_copy(
            src_ref=log_out.at[peer], dst_ref=log_in.at[source],
            send_sem=log_send.at[offset - 1], recv_sem=log_recv.at[source],
            device_id={"head": peer}, device_id_type=pl.DeviceIdType.MESH,
        )

    for copy in load(0):
        copy.start()
    barrier = pltpu.get_barrier_semaphore()
    for offset in range(1, n_head):
        pl.semaphore_signal(
            barrier, inc=1, device_id={"head": peer_of(me, n_head, offset)},
            device_id_type=pl.DeviceIdType.MESH,
        )
    for offset in range(1, n_cache):
        pl.semaphore_signal(
            barrier, inc=1, device_id={"cache": peer_of(seat, n_cache, offset)},
            device_id_type=pl.DeviceIdType.MESH,
        )
    for block in range(head_blocks):
        own_query(block).start()
    pl.semaphore_wait(barrier, n_head + n_cache - 2)
    for offset in range(1, n_head):
        query_copy(0, offset, me).start()
    log_out[...] = jnp.zeros_like(log_out)
    slots = lists.shape[1]
    used = lax.broadcasted_iota(jnp.int32, (1, slots), 1) < counts[0]
    listed = jnp.where(used, lists[...], -1)
    match = listed == lax.broadcasted_iota(jnp.int32, (pages, slots), 0)
    cap = jnp.max(jnp.where(match, highest, lowest), axis=1, keepdims=True)
    caps[...] = jnp.broadcast_to(cap, caps.shape)

    def ready(block):
        for copy in load(block):
            copy.wait()
        own_query(block).wait()
        for offset in range(1, n_head):
            query_copy(block, offset, peer_of(me, n_head, offset)).wait_recv()

        @pl.when(block + 1 < head_blocks)
        def _():
            for copy in load(block + 1):
                copy.start()
            for offset in range(1, n_head):
                query_copy(block + 1, offset, me).start()

    def compute(group):
        block = group // tile_blocks
        if tile_blocks == 1:
            ready(block)
        else:
            pl.when(group % tile_blocks == 0)(lambda: ready(block))

        def column(unit):
            return slice(unit // tiles_in * DH, (unit // tiles_in + 1) * DH)

        for unit in range(units):
            first = (group % tile_blocks * tiles_in + unit % tiles_in) * sources
            rows = [q_all[block, first + l, :, column(unit)].astype(jnp.float32) for l in range(sources)]
            ordered = [
                row[c * share:(c + 1) * share] for c in range(n_cache) for row in rows
            ]
            q_units[unit] = jnp.concatenate(ordered, axis=0).astype(jnp.bfloat16)
        bests = attend(
            [q_units.at[unit] for unit in range(units)],
            lambda unit, page: k_buf[block, page, :, column(unit)],
            lambda unit, page: v_buf[block, page, :, column(unit)],
            caps, pages, acc, scores,
        )
        row = lax.broadcasted_iota(jnp.int32, (8, TILE), 0)
        tails = [jnp.where(row == 1, best, acc[unit, DH:ROWS]) for unit, best in enumerate(bests)]
        for member in range(n_cache):
            piece = slice(member * chunk, (member + 1) * chunk)
            part_out[group, member, :DH] = jnp.concatenate(
                [acc[unit, :DH, piece] for unit in range(units)], axis=1
            )
            part_out[group, member, DH:ROWS] = jnp.concatenate([tail[:, piece] for tail in tails], axis=1)
        for offset in range(1, n_cache):
            part_copy(group, offset, seat).start()
        part_in[group, seat] = part_out[group, seat]

    def finish(group):
        block = group // tile_blocks
        for offset in range(1, n_cache):
            part_copy(group, offset, peer_of(seat, n_cache, offset)).wait_recv()
        totals = [part_in[group, c, DH:DH + 1] for c in range(n_cache)]
        bests = [part_in[group, c, DH + 1:DH + 2] for c in range(n_cache)]
        top = functools.reduce(jnp.maximum, bests)
        keeps = [jnp.exp2((best - top) * LOG2_SCALE) for best in bests]
        total = functools.reduce(jnp.add, [t * keep for t, keep in zip(totals, keeps)])
        inverse = 1.0 / total
        result = functools.reduce(
            jnp.add, [part_in[group, c, :DH] * (keep * inverse) for c, keep in enumerate(keeps)]
        ).T
        logged = jnp.broadcast_to(top * SCALE + jnp.log(total), (LANES, LANES)).T
        lane = lax.broadcasted_iota(jnp.int32, (share, LANES), 1)
        for unit in range(units):
            head = unit // tiles_in
            for l in range(sources):
                place = unit % tiles_in * sources + l
                at = unit * sources * share + l * share
                piece_out[group, place, :, head * DH:(head + 1) * DH] = result[at:at + share]
                target = group % tile_blocks * spread + place
                log_out[target] += jnp.where(
                    lane == me * heads + block * heads_in + head, logged[at:at + share], 0.0
                )
        for place in range(spread):
            target, copy = piece_copy(group, place, me)
            pl.when(target != me)(copy.start)

            @pl.when(target == me)
            def _():
                piece_in[block, me] = piece_out[group, place]

    def step(group, carry):
        compute(group)
        pl.when(group > 0)(lambda: finish(group - 1))
        return carry

    lax.fori_loop(0, groups, step, 0)
    finish(groups - 1)
    for offset in range(1, n_head):
        log_copy(offset, me).start()
    log_in[me] = log_out[me]
    for block in range(head_blocks):
        for offset in range(1, n_head):
            query_copy(block, offset, me).wait_send()
    for group in range(groups):
        for offset in range(1, n_cache):
            part_copy(group, offset, seat).wait_send()
    for block in range(head_blocks):
        for offset in range(1, n_head):
            source = peer_of(me, n_head, offset)
            pltpu.make_async_remote_copy(
                src_ref=piece_out.at[block, 0], dst_ref=piece_in.at[block, source],
                send_sem=piece_send.at[block, 0], recv_sem=piece_recv.at[block, source],
                device_id={"head": source}, device_id_type=pl.DeviceIdType.MESH,
            ).wait_recv()
        for source in range(n_head):
            at = (source * heads + block * heads_in) * DH
            out_ref[:, at:at + width] = piece_in[block, source]
    for offset in range(1, n_head):
        log_copy(offset, peer_of(me, n_head, offset)).wait_recv()
    log_ref[...] = functools.reduce(jnp.add, [log_in[s] for s in range(n_head)])[:, :log_ref.shape[1]]
    for group in range(groups):
        for place in range(spread):
            target, copy = piece_copy(group, place, me)
            pl.when(target != me)(copy.wait_send)
    for offset in range(1, n_head):
        log_copy(offset, me).wait_send()


def settle(attended, logged, out_ref, log_ref, sem):
    copies = (
        pltpu.make_async_copy(attended, out_ref, sem.at[0]),
        pltpu.make_async_copy(logged, log_ref, sem.at[1]),
    )
    for copy in copies:
        copy.start()
    for copy in copies:
        copy.wait()


def on_device(queries, keys, values, page_lists, page_counts):
    n_head = lax.axis_size("head")
    n_cache = lax.axis_size("cache")
    tok_local = queries.shape[0]
    heads = keys.shape[2] // DH
    pages = keys.shape[0]
    share = tok_local // n_cache
    sources = TILE // tok_local
    tiles = n_head // sources
    units = LANES * n_cache // TILE
    tiles_in = min(units, tiles)
    heads_in = units // tiles_in
    tile_blocks = tiles // tiles_in
    head_blocks = heads // heads_in
    groups = head_blocks * tile_blocks
    spread = tiles_in * sources
    width = heads_in * DH
    plan = (groups, heads_in, tiles_in, tile_blocks, n_head, n_cache, heads, sources)
    dma = pltpu.SemaphoreType.DMA
    attended, logged = pl.pallas_call(
        functools.partial(kernel, plan),
        out_shape=(
            jax.ShapeDtypeStruct((share, queries.shape[1]), jnp.float32),
            jax.ShapeDtypeStruct((share, n_head * heads), jnp.float32),
        ),
        in_specs=[
            pl.BlockSpec(memory_space=pltpu.VMEM),
            pl.BlockSpec(memory_space=pl.ANY),
            pl.BlockSpec(memory_space=pl.ANY),
            pl.BlockSpec(memory_space=pltpu.VMEM),
            pl.BlockSpec(memory_space=pltpu.SMEM),
        ],
        out_specs=(pl.BlockSpec(memory_space=pltpu.VMEM), pl.BlockSpec(memory_space=pltpu.VMEM)),
        scratch_shapes=[
            pltpu.VMEM((pages, TILE), jnp.float32),
            pltpu.VMEM((head_blocks, pages, PAGE, width), jnp.bfloat16),
            pltpu.VMEM((head_blocks, pages, PAGE, width), jnp.bfloat16),
            pltpu.VMEM((head_blocks, n_head, tok_local, width), jnp.bfloat16),
            pltpu.VMEM((units, TILE, DH), jnp.bfloat16),
            pltpu.VMEM((units, ROWS, TILE), jnp.float32),
            pltpu.VMEM((units, BLOCK, PAGE, TILE), jnp.float32),
            pltpu.VMEM((groups, n_cache, ROWS, LANES), jnp.float32),
            pltpu.VMEM((groups, n_cache, ROWS, LANES), jnp.float32),
            pltpu.VMEM((groups, spread, share, width), jnp.float32),
            pltpu.VMEM((head_blocks, n_head, share, width), jnp.float32),
            pltpu.VMEM((n_head, share, LANES), jnp.float32),
            pltpu.VMEM((n_head, share, LANES), jnp.float32),
            dma((head_blocks,)),
            dma((head_blocks,)),
            dma((head_blocks,)),
            dma((head_blocks, n_head - 1)),
            dma((head_blocks, n_head)),
            dma((groups, n_cache - 1)),
            dma((groups, n_cache)),
            dma((groups, spread)),
            dma((head_blocks, n_head)),
            dma((n_head - 1,)),
            dma((n_head,)),
        ],
        compiler_params=pltpu.CompilerParams(
            collective_id=0, has_side_effects=True, vmem_limit_bytes=56 * 1024 * 1024
        ),
    )(queries, keys, values, page_lists, page_counts)
    any_place = pl.BlockSpec(memory_space=pl.ANY)
    return pl.pallas_call(
        settle,
        out_shape=(
            jax.ShapeDtypeStruct(attended.shape, jnp.float32),
            jax.ShapeDtypeStruct(logged.shape, jnp.float32),
        ),
        in_specs=[pl.BlockSpec(memory_space=pltpu.VMEM)] * 2,
        out_specs=(any_place, any_place),
        scratch_shapes=[dma((2,))],
    )(attended, logged)


def solution(mesh):
    in_specs = (
        P(("group", "head"), None),
        P(("group", "cache"), None, "head"),
        P(("group", "cache"), None, "head"),
        P(("group", "cache"), None),
        P(("group", "cache")),
    )
    out_specs = (P(("group", "head", "cache"), None), P(("group", "head", "cache"), None))
    return jax.shard_map(
        on_device, mesh=mesh, in_specs=in_specs, out_specs=out_specs, check_vma=False
    )
```

```python
import functools
import math

import jax
import jax.numpy as jnp
from jax import lax
from jax.experimental import pallas as pl
from jax.experimental.pallas import tpu as pltpu
from jax.sharding import PartitionSpec as P

DH = 128
PAGE = 128
LANES = 128
TILE = 256
ROWS = DH + 8
BLOCK = 8
SCALE = 1.0 / math.sqrt(DH)
LOG2_SCALE = SCALE * math.log2(math.e)

lowest = -1e30
highest = 3e38


def attend(queries, key_of, value_of, caps, pages, acc, scores):
    units = len(queries)
    acc[...] = jnp.zeros_like(acc)
    ones = jnp.ones((16, PAGE), jnp.bfloat16)
    blocks = pages // BLOCK

    def score(unit, page):
        rows = key_of(unit, pl.ds(page, BLOCK)).reshape(BLOCK * PAGE, DH)
        return lax.dot_general(
            rows, queries[unit][...], (((1,), (1,)), ((), ())),
            preferred_element_type=jnp.float32,
        ).reshape(BLOCK, PAGE, TILE)

    for unit in range(units):
        scores[unit] = score(unit, 0)

    def visit(block, bests, more=True):
        runnings = []
        for unit in range(units):
            maxima, outs = [], []
            for step in range(BLOCK):
                page = block * BLOCK + step
                page_max = jnp.max(scores[unit, step], axis=0, keepdims=True)
                weights = jnp.exp2((scores[unit, step] - page_max) * LOG2_SCALE).astype(jnp.bfloat16)
                left = jnp.concatenate([value_of(unit, page).T, ones], axis=0)
                outs.append(jnp.dot(left, weights, preferred_element_type=jnp.float32)[:ROWS])
                maxima.append(jnp.minimum(page_max, caps[pl.ds(page, 1), :]))
            if more:
                scores[unit] = score(unit, (block + 1) * BLOCK)
            running = functools.reduce(jnp.maximum, maxima, bests[unit])
            joined = acc[unit] * jnp.exp2((bests[unit] - running) * LOG2_SCALE)
            for used_max, out in zip(maxima, outs):
                joined += out * jnp.exp2((used_max - running) * LOG2_SCALE)
            acc[unit] = joined
            runnings.append(running)
        return tuple(runnings)

    start = jnp.full((1, TILE), lowest, jnp.float32)
    bests = lax.fori_loop(0, blocks - 1, visit, (start,) * units)
    return visit(blocks - 1, bests, more=False)


def kernel(
    plan, q_ref, k_hbm, v_hbm, lists, counts, out_ref, log_ref,
    caps, k_buf, v_buf, q_all, q_units, acc, scores, part_out, part_in, piece_out, piece_in, log_out, log_in,
    k_sem, v_sem, own_sem, q_send, q_recv, part_send, part_recv, piece_send, piece_recv, log_send, log_recv,
):
    groups, heads_in, tiles_in, tile_blocks, n_head, n_cache, heads, sources = plan
    units = heads_in * tiles_in
    width = heads_in * DH
    pages = k_hbm.shape[0]
    head_blocks = groups // tile_blocks
    share = q_ref.shape[0] // n_cache
    chunk = TILE // n_cache
    spread = tiles_in * sources
    me = lax.axis_index("head")
    seat = lax.axis_index("cache")

    def load(block):
        columns = pl.ds(pl.multiple_of(block * width, DH), width)
        return (
            pltpu.make_async_copy(k_hbm.at[:, :, columns], k_buf.at[block], k_sem.at[block]),
            pltpu.make_async_copy(v_hbm.at[:, :, columns], v_buf.at[block], v_sem.at[block]),
        )

    def peer_of(index, count, offset):
        return lax.rem(index + offset, count)

    def query_source(block, owner):
        return q_ref.at[:, pl.ds(pl.multiple_of(owner * heads * DH + block * width, DH), width)]

    def own_query(block):
        return pltpu.make_async_copy(query_source(block, me), q_all.at[block, me], own_sem.at[block])

    def query_copy(block, offset, source):
        peer = peer_of(me, n_head, offset)
        return pltpu.make_async_remote_copy(
            src_ref=query_source(block, peer), dst_ref=q_all.at[block, source],
            send_sem=q_send.at[block, offset - 1], recv_sem=q_recv.at[block, source],
            device_id={"head": peer}, device_id_type=pl.DeviceIdType.MESH,
        )

    def part_copy(group, offset, source):
        peer = peer_of(seat, n_cache, offset)
        return pltpu.make_async_remote_copy(
            src_ref=part_out.at[group, peer], dst_ref=part_in.at[group, source],
            send_sem=part_send.at[group, offset - 1], recv_sem=part_recv.at[group, source],
            device_id={"cache": peer}, device_id_type=pl.DeviceIdType.MESH,
        )

    def piece_copy(group, place, source):
        target = group % tile_blocks * spread + place
        block = group // tile_blocks
        return target, pltpu.make_async_remote_copy(
            src_ref=piece_out.at[group, place], dst_ref=piece_in.at[block, source],
            send_sem=piece_send.at[group, place], recv_sem=piece_recv.at[block, source],
            device_id={"head": target}, device_id_type=pl.DeviceIdType.MESH,
        )

    def log_copy(offset, source):
        peer = peer_of(me, n_head, offset)
        return pltpu.make_async_remote_copy(
            src_ref=log_out.at[peer], dst_ref=log_in.at[source],
            send_sem=log_send.at[offset - 1], recv_sem=log_recv.at[source],
            device_id={"head": peer}, device_id_type=pl.DeviceIdType.MESH,
        )

    for copy in load(0):
        copy.start()
    barrier = pltpu.get_barrier_semaphore()
    for offset in range(1, n_head):
        pl.semaphore_signal(
            barrier, inc=1, device_id={"head": peer_of(me, n_head, offset)},
            device_id_type=pl.DeviceIdType.MESH,
        )
    for offset in range(1, n_cache):
        pl.semaphore_signal(
            barrier, inc=1, device_id={"cache": peer_of(seat, n_cache, offset)},
            device_id_type=pl.DeviceIdType.MESH,
        )
    for block in range(head_blocks):
        own_query(block).start()
    pl.semaphore_wait(barrier, n_head + n_cache - 2)
    for offset in range(1, n_head):
        query_copy(0, offset, me).start()
    log_out[...] = jnp.zeros_like(log_out)
    slots = lists.shape[1]
    used = lax.broadcasted_iota(jnp.int32, (1, slots), 1) < counts[0]
    listed = jnp.where(used, lists[...], -1)
    match = listed == lax.broadcasted_iota(jnp.int32, (pages, slots), 0)
    cap = jnp.max(jnp.where(match, highest, lowest), axis=1, keepdims=True)
    caps[...] = jnp.broadcast_to(cap, caps.shape)

    def ready(block):
        for copy in load(block):
            copy.wait()
        own_query(block).wait()
        for offset in range(1, n_head):
            query_copy(block, offset, peer_of(me, n_head, offset)).wait_recv()

        @pl.when(block + 1 < head_blocks)
        def _():
            for copy in load(block + 1):
                copy.start()
            for offset in range(1, n_head):
                query_copy(block + 1, offset, me).start()

    def compute(group):
        block = group // tile_blocks
        if tile_blocks == 1:
            ready(block)
        else:
            pl.when(group % tile_blocks == 0)(lambda: ready(block))

        def column(unit):
            return slice(unit // tiles_in * DH, (unit // tiles_in + 1) * DH)

        for unit in range(units):
            first = (group % tile_blocks * tiles_in + unit % tiles_in) * sources
            rows = [q_all[block, first + l, :, column(unit)].astype(jnp.float32) for l in range(sources)]
            ordered = [
                row[c * share:(c + 1) * share] for c in range(n_cache) for row in rows
            ]
            q_units[unit] = jnp.concatenate(ordered, axis=0).astype(jnp.bfloat16)
        bests = attend(
            [q_units.at[unit] for unit in range(units)],
            lambda unit, page: k_buf[block, page, :, column(unit)],
            lambda unit, page: v_buf[block, page, :, column(unit)],
            caps, pages, acc, scores,
        )
        row = lax.broadcasted_iota(jnp.int32, (8, TILE), 0)
        tails = [jnp.where(row == 1, best, acc[unit, DH:ROWS]) for unit, best in enumerate(bests)]
        for member in range(n_cache):
            piece = slice(member * chunk, (member + 1) * chunk)
            part_out[group, member, :DH] = jnp.concatenate(
                [acc[unit, :DH, piece] for unit in range(units)], axis=1
            )
            part_out[group, member, DH:ROWS] = jnp.concatenate([tail[:, piece] for tail in tails], axis=1)
        for offset in range(1, n_cache):
            part_copy(group, offset, seat).start()
        part_in[group, seat] = part_out[group, seat]

    def finish(group):
        block = group // tile_blocks
        for offset in range(1, n_cache):
            part_copy(group, offset, peer_of(seat, n_cache, offset)).wait_recv()
        totals = [part_in[group, c, DH:DH + 1] for c in range(n_cache)]
        bests = [part_in[group, c, DH + 1:DH + 2] for c in range(n_cache)]
        top = functools.reduce(jnp.maximum, bests)
        keeps = [jnp.exp2((best - top) * LOG2_SCALE) for best in bests]
        total = functools.reduce(jnp.add, [t * keep for t, keep in zip(totals, keeps)])
        inverse = 1.0 / total
        result = functools.reduce(
            jnp.add, [part_in[group, c, :DH] * (keep * inverse) for c, keep in enumerate(keeps)]
        ).T
        logged = jnp.broadcast_to(top * SCALE + jnp.log(total), (LANES, LANES)).T
        lane = lax.broadcasted_iota(jnp.int32, (share, LANES), 1)
        for unit in range(units):
            head = unit // tiles_in
            for l in range(sources):
                place = unit % tiles_in * sources + l
                at = unit * sources * share + l * share
                piece_out[group, place, :, head * DH:(head + 1) * DH] = result[at:at + share]
                target = group % tile_blocks * spread + place
                log_out[target] += jnp.where(
                    lane == me * heads + block * heads_in + head, logged[at:at + share], 0.0
                )
        for place in range(spread):
            target, copy = piece_copy(group, place, me)
            pl.when(target != me)(copy.start)

            @pl.when(target == me)
            def _():
                piece_in[block, me] = piece_out[group, place]

    def step(group, carry):
        compute(group)
        pl.when(group > 0)(lambda: finish(group - 1))
        return carry

    lax.fori_loop(0, groups, step, 0)
    finish(groups - 1)
    for offset in range(1, n_head):
        log_copy(offset, me).start()
    log_in[me] = log_out[me]
    for block in range(head_blocks):
        for offset in range(1, n_head):
            query_copy(block, offset, me).wait_send()
    for group in range(groups):
        for offset in range(1, n_cache):
            part_copy(group, offset, seat).wait_send()
    for block in range(head_blocks):
        for offset in range(1, n_head):
            source = peer_of(me, n_head, offset)
            pltpu.make_async_remote_copy(
                src_ref=piece_out.at[block, 0], dst_ref=piece_in.at[block, source],
                send_sem=piece_send.at[block, 0], recv_sem=piece_recv.at[block, source],
                device_id={"head": source}, device_id_type=pl.DeviceIdType.MESH,
            ).wait_recv()
        for source in range(n_head):
            at = (source * heads + block * heads_in) * DH
            out_ref[:, at:at + width] = piece_in[block, source]
    for offset in range(1, n_head):
        log_copy(offset, peer_of(me, n_head, offset)).wait_recv()
    log_ref[...] = functools.reduce(jnp.add, [log_in[s] for s in range(n_head)])[:, :log_ref.shape[1]]
    for group in range(groups):
        for place in range(spread):
            target, copy = piece_copy(group, place, me)
            pl.when(target != me)(copy.wait_send)
    for offset in range(1, n_head):
        log_copy(offset, me).wait_send()


def on_device(queries, keys, values, page_lists, page_counts):
    n_head = lax.axis_size("head")
    n_cache = lax.axis_size("cache")
    tok_local = queries.shape[0]
    heads = keys.shape[2] // DH
    pages = keys.shape[0]
    share = tok_local // n_cache
    sources = TILE // tok_local
    tiles = n_head // sources
    units = LANES * n_cache // TILE
    tiles_in = min(units, tiles)
    heads_in = units // tiles_in
    tile_blocks = tiles // tiles_in
    head_blocks = heads // heads_in
    groups = head_blocks * tile_blocks
    spread = tiles_in * sources
    width = heads_in * DH
    plan = (groups, heads_in, tiles_in, tile_blocks, n_head, n_cache, heads, sources)
    dma = pltpu.SemaphoreType.DMA
    attended, logged = pl.pallas_call(
        functools.partial(kernel, plan),
        out_shape=(
            pltpu.VMEM((share, queries.shape[1]), jnp.float32),
            pltpu.VMEM((share, n_head * heads), jnp.float32),
        ),
        in_specs=[
            pl.BlockSpec(memory_space=pltpu.VMEM),
            pl.BlockSpec(memory_space=pl.ANY),
            pl.BlockSpec(memory_space=pl.ANY),
            pl.BlockSpec(memory_space=pltpu.VMEM),
            pl.BlockSpec(memory_space=pltpu.SMEM),
        ],
        out_specs=(pl.BlockSpec(memory_space=pltpu.VMEM), pl.BlockSpec(memory_space=pltpu.VMEM)),
        scratch_shapes=[
            pltpu.VMEM((pages, TILE), jnp.float32),
            pltpu.VMEM((head_blocks, pages, PAGE, width), jnp.bfloat16),
            pltpu.VMEM((head_blocks, pages, PAGE, width), jnp.bfloat16),
            pltpu.VMEM((head_blocks, n_head, tok_local, width), jnp.bfloat16),
            pltpu.VMEM((units, TILE, DH), jnp.bfloat16),
            pltpu.VMEM((units, ROWS, TILE), jnp.float32),
            pltpu.VMEM((units, BLOCK, PAGE, TILE), jnp.float32),
            pltpu.VMEM((groups, n_cache, ROWS, LANES), jnp.float32),
            pltpu.VMEM((groups, n_cache, ROWS, LANES), jnp.float32),
            pltpu.VMEM((groups, spread, share, width), jnp.float32),
            pltpu.VMEM((head_blocks, n_head, share, width), jnp.float32),
            pltpu.VMEM((n_head, share, LANES), jnp.float32),
            pltpu.VMEM((n_head, share, LANES), jnp.float32),
            dma((head_blocks,)),
            dma((head_blocks,)),
            dma((head_blocks,)),
            dma((head_blocks, n_head - 1)),
            dma((head_blocks, n_head)),
            dma((groups, n_cache - 1)),
            dma((groups, n_cache)),
            dma((groups, spread)),
            dma((head_blocks, n_head)),
            dma((n_head - 1,)),
            dma((n_head,)),
        ],
        compiler_params=pltpu.CompilerParams(
            collective_id=0, has_side_effects=True, vmem_limit_bytes=56 * 1024 * 1024
        ),
    )(queries, keys, values, page_lists, page_counts)
    return attended, logged


def solution(mesh):
    in_specs = (
        P(("group", "head"), None),
        P(("group", "cache"), None, "head"),
        P(("group", "cache"), None, "head"),
        P(("group", "cache"), None),
        P(("group", "cache")),
    )
    out_specs = (P(("group", "head", "cache"), None), P(("group", "head", "cache"), None))
    return jax.shard_map(
        on_device, mesh=mesh, in_specs=in_specs, out_specs=out_specs, check_vma=False
    )
```
